32 devices in a mesh: cp: 8 (over z, y), tp: 4 (over x, core).
Axes of the slice: x: 2, y: 2, z: 4, core: 2. Of those that a mesh axis runs over, the one named last changes fastest.
Arguments:
- queries: bfloat16 [1024, 8, 16, 128], P('cp', None, 'tp'), may hold values from -64 to 64
- key_heads: bfloat16 [1024, 8, 128], P('cp', 'tp'), may hold values from -6 to 6
- value_heads: bfloat16 [1024, 8, 128], P('cp', 'tp'), may hold values from -6 to 6
- grad_out: bfloat16 [1024, 8, 16, 128], P('cp', None, 'tp'), may hold values from -6 to 6
- doc_starts: int32 [1024], replicated, may hold values from 0 to 1024, as said below
Outputs:
- grad_queries: bfloat16 [1024, 8, 16, 128], P('cp', None, 'tp')
- grad_keys: bfloat16 [1024, 8, 128], P('cp', 'tp')
- grad_values: bfloat16 [1024, 8, 128], P('cp', 'tp')
The draws below stay inside these ranges and needn't reach their ends.
Inputs may be any that keep to these rules, and one draw needn't show every extreme that they name: doc_starts does not fall and doc_starts[0] = 0; the documents are the nonempty runs from one entry to the next (the last to 1024); each has 1 to 384 tokens, the first has exactly 384; entries after the last document's start equal 1024.
All inputs are finite; a program needn't handle non-finite values.
Results may differ from the reference program's by a relative error of at most 0.011.
Values may be sent and summed in bfloat16 or wider, within the bound.
A program may use at most 64 MiB of HBM per device.

```python
import jax
import jax.numpy as jnp
from jax import lax

KVH = 8
GROUP = 16
HD = 128
TOK_DEV = 128
REACH = 3
MAXDOC = 384
TOKENS = 1024
N_CP = 8


def make_starts(seed_key):
    lengths = jax.random.randint(jax.random.fold_in(seed_key, 1), (TOKENS,), 1, MAXDOC + 1)
    long_doc = jax.random.randint(jax.random.fold_in(seed_key, 2), (), 0, TOKENS // MAXDOC)
    lengths = jnp.where(jnp.arange(TOKENS) == long_doc, MAXDOC, lengths)
    lengths = jnp.where(jnp.arange(TOKENS) == 0, MAXDOC, lengths)
    starts = jnp.cumsum(lengths) - lengths
    return jnp.minimum(starts, TOKENS).astype(jnp.int32)


def draw_pair(seed_key):
    key_draw = jnp.clip(jax.random.normal(jax.random.fold_in(seed_key, 21), (TOKENS, KVH, HD), jnp.float32), -6.0, 6.0)
    query_draw = jnp.clip(jax.random.normal(jax.random.fold_in(seed_key, 22), (TOKENS, KVH, GROUP, HD), jnp.float32), -6.0, 6.0)
    return (query_draw, key_draw)


def draw_doc_starts(key, part):
    return make_starts(jax.random.fold_in(key, 11))


def draw_queries(key, part):
    return draw_pair(key)[0].astype(jnp.bfloat16)


def draw_key_heads(key, part):
    return draw_pair(key)[1].astype(jnp.bfloat16)


def level_of(stream_key, extent, shards, smallest, largest):
    loudness, own = 1.0, jax.random.fold_in(stream_key, 6)
    for dim, blocks in shards:
        draws = jnp.exp(jax.random.uniform(jax.random.fold_in(own, dim), (blocks,), jnp.float32, smallest / len(shards), largest / len(shards)))
        loudness = loudness * jnp.repeat(draws, extent[dim] // blocks).reshape([-1 if axis == dim else 1 for axis in range(len(extent))])
    return loudness


def noise(own_key, extent, deviation, reach, cuts=(), held_as=jnp.bfloat16):
    level = level_of(own_key, extent, cuts, -0.22, 0.18) if cuts else 1.0
    array = jax.random.normal(own_key, extent, jnp.float32) * deviation * level
    return jnp.minimum(jnp.maximum(array, -reach), reach).astype(held_as)


def setup_inputs(seed: int = 0) -> dict:
    streams_of = jax.random.split(jax.random.key(seed), 6)
    return {
        "queries": draw_queries(jax.random.fold_in(streams_of[5], 71), 0),
        "key_heads": draw_key_heads(jax.random.fold_in(streams_of[5], 71), 0),
        "value_heads": noise(streams_of[2], (TOKENS, KVH, HD), 1.0, 6.0, ((0, 8), (1, 4))),
        "grad_out": noise(streams_of[3], (TOKENS, KVH, GROUP, HD), 1.0, 6.0, ((0, 8), (2, 4))),
        "doc_starts": draw_doc_starts(jax.random.fold_in(streams_of[5], 71), 0),
    }


MASKED_LOGIT = -1.0e30


def reference(queries, key_heads, value_heads, grad_out, doc_starts):
    scaling = HD ** -0.5
    key_span = (REACH + 1) * TOK_DEV
    margin = REACH * TOK_DEV
    highest = lax.Precision.HIGHEST
    row_ids = jnp.arange(TOKENS, dtype=jnp.int32)
    doc_ids = (jnp.searchsorted(doc_starts, row_ids, side="right") - 1).astype(jnp.int32)
    lead_keys = jnp.concatenate([jnp.zeros((margin, KVH, HD), key_heads.dtype), key_heads], axis=0)
    lead_values = jnp.concatenate([jnp.zeros((margin, KVH, HD), value_heads.dtype), value_heads], axis=0)
    lead_docs = jnp.concatenate([jnp.full((margin,), -1, jnp.int32), doc_ids])
    lead_pos = jnp.concatenate([jnp.full((margin,), -1, jnp.int32), row_ids])

    def per_block(carried, block_index):
        grad_keys, grad_values = carried
        first_row = (block_index * TOK_DEV).astype(jnp.int32)
        query_blk = lax.dynamic_slice_in_dim(queries, first_row, TOK_DEV, 0).astype(jnp.float32)
        out_blk = lax.dynamic_slice_in_dim(grad_out, first_row, TOK_DEV, 0).astype(jnp.float32)
        key_blk = lax.dynamic_slice_in_dim(lead_keys, first_row, key_span, 0).astype(jnp.float32)
        value_blk = lax.dynamic_slice_in_dim(lead_values, first_row, key_span, 0).astype(jnp.float32)
        query_doc = lax.dynamic_slice_in_dim(doc_ids, first_row, TOK_DEV, 0)
        query_pos = lax.dynamic_slice_in_dim(row_ids, first_row, TOK_DEV, 0)
        key_doc = lax.dynamic_slice_in_dim(lead_docs, first_row, key_span, 0)
        key_pos = lax.dynamic_slice_in_dim(lead_pos, first_row, key_span, 0)
        allowed = (key_doc[None, :] == query_doc[:, None]) & (key_pos[None, :] <= query_pos[:, None])
        allowed = allowed[None, None]
        logits = scaling * jnp.einsum("ighc,jgc->ghij", query_blk, key_blk, precision=highest)
        row_peak = jnp.max(jnp.where(allowed, logits, MASKED_LOGIT), axis=-1)
        weights = jnp.where(allowed, jnp.exp(logits - row_peak[..., None]), 0.0)
        row_total = jnp.sum(weights, axis=-1)
        grad_prob = jnp.einsum("ighc,jgc->ghij", out_blk, value_blk, precision=highest)
        row_delta = jnp.sum(weights * grad_prob, axis=-1) / row_total
        log_total = row_peak + jnp.log(row_total)
        probs = jnp.where(allowed, jnp.exp(logits - log_total[..., None]), 0.0)
        probs_half = lax.optimization_barrier(probs.astype(jnp.bfloat16)).astype(jnp.float32)
        grad_logit = (probs * (grad_prob - row_delta[..., None])).astype(jnp.bfloat16)
        grad_logit = lax.optimization_barrier(grad_logit).astype(jnp.float32)
        grad_query = scaling * jnp.einsum("ghij,jgc->ighc", grad_logit, key_blk, precision=highest)
        more_keys = scaling * jnp.einsum("ghij,ighc->jgc", grad_logit, query_blk, precision=highest)
        more_values = jnp.einsum("ghij,ighc->jgc", probs_half, out_blk, precision=highest)
        current_k = lax.dynamic_slice_in_dim(grad_keys, first_row, key_span, 0)
        current_v = lax.dynamic_slice_in_dim(grad_values, first_row, key_span, 0)
        grad_keys = lax.dynamic_update_slice_in_dim(grad_keys, current_k + more_keys, first_row, 0)
        grad_values = lax.dynamic_update_slice_in_dim(grad_values, current_v + more_values, first_row, 0)
        return (grad_keys, grad_values), grad_query.astype(jnp.bfloat16)

    zeros_kv = jnp.zeros((TOKENS + margin, KVH, HD), jnp.float32)
    finished, grad_query = lax.scan(per_block, (zeros_kv, zeros_kv), jnp.arange(N_CP, dtype=jnp.int32))
    grad_keys, grad_values = finished
    grad_query = grad_query.reshape(TOKENS, KVH, GROUP, HD)
    return grad_query, grad_keys[margin:].astype(jnp.bfloat16), grad_values[margin:].astype(jnp.bfloat16)
```

```python
import functools
import math

import jax
import jax.numpy as jnp
from jax import lax
from jax.experimental import pallas as pl
from jax.experimental.pallas import tpu as pltpu
from jax.sharding import PartitionSpec as P

REACH = 3
FIRST_DOC = 384
NEG = -1e30
MESH = pl.DeviceIdType.MESH
F32 = jnp.float32
BF16 = jnp.bfloat16
NT = (((1,), (1,)), ((), ()))


def dot(a, b):
    return jnp.dot(a, b, preferred_element_type=F32)


def dot_nt(a, b):
    return lax.dot_general(a, b, NT, preferred_element_type=F32)


def kernel(
    n_cp, n_tp, heads, chunk,
    q_ref, do_ref, kv_ref, starts_ref,
    dq_ref, dkv_ref,
    win, bias, p0, pb, r1, r2, r3, ts, fb,
    rs_w, rs_f, ss_1, ss_2, ss_3, ss_4, rs_1, rs_2, rs_3, sb_1, sb_2, sb_3, sb_f,
):
    me = lax.axis_index("cp")
    t = lax.axis_index("tp")
    hps, _, tok, dim = kv_ref.shape
    rows = q_ref.shape[1]
    span = (REACH + 1) * tok
    lead = FIRST_DOC // tok
    scaling = dim ** (-0.5)
    peer = (t, t + 1 - 2 * (t % 2), (t + n_tp // 2) % n_tp, n_tp - 1 - t)

    def sees(i, d):
        return (i - d >= 0) & ((i < lead) | (i - d >= lead))

    def gets(d):
        return sees(me, d)

    def gives(d):
        return (me + d < n_cp) & sees(me + d, d)

    def copy(src, dst, send, recv, where):
        return pltpu.make_async_remote_copy(
            src_ref=src, dst_ref=dst, send_sem=send, recv_sem=recv,
            device_id=where, device_id_type=MESH,
        )

    def to_cp(i):
        return {"cp": i}

    def to_tp(s):
        return {"tp": peer[s]}

    def f1(h, d):
        return copy(kv_ref.at[h], win.at[0, h, d], ss_1.at[h, d], rs_w.at[0, h, d], to_cp(me + d))

    def f_src(h, d):
        return kv_ref.at[h] if d == 0 else win.at[0, h, d]

    def f2(h, d):
        return copy(f_src(h, d), win.at[1, h, d], ss_2.at[h, d], rs_w.at[1, h, d], to_tp(1))

    def f3(h, d):
        return copy(f_src(h, d), win.at[2, h, d], ss_3.at[h, d], rs_w.at[2, h, d], to_tp(2))

    def f4(h, d):
        return copy(win.at[2, h, d], win.at[3, h, d], ss_4.at[h, d], rs_w.at[3, h, d], to_tp(1))

    def b1(h):
        return copy(pb.at[1, h], r1.at[h], sb_1.at[h], rs_1.at[h], to_tp(1))

    def b2(h):
        return copy(pb.at[2, h], r2.at[h], sb_2.at[h], rs_2.at[h], to_tp(2))

    def b3(h):
        return copy(pb.at[3, h], r3.at[h], sb_3.at[h], rs_3.at[h], to_tp(1))

    def bf(h, d):
        return copy(ts.at[h, d], fb.at[h, d], sb_f.at[h, d], rs_f.at[h, d], to_cp(me - d))

    def when_d(cond, d, action):
        if d == 0:
            action()
        else:
            pl.when(cond(d))(action)

    barrier = pltpu.get_barrier_semaphore()
    for s in (1, 2):
        pl.semaphore_signal(barrier, inc=1, device_id=to_tp(s), device_id_type=MESH)
    count = jnp.int32(2)
    for d in range(1, REACH + 1):
        count += gets(d).astype(jnp.int32) + gives(d).astype(jnp.int32)

        @pl.when(gets(d))
        def _():
            pl.semaphore_signal(barrier, inc=1, device_id=to_cp(me - d), device_id_type=MESH)

        @pl.when(gives(d))
        def _():
            pl.semaphore_signal(barrier, inc=1, device_id=to_cp(me + d), device_id_type=MESH)

    pl.semaphore_wait(barrier, count)

    for h in range(hps):
        f3(h, 0).start()
        for d in range(1, REACH + 1):
            pl.when(gives(d))(lambda: f1(h, d).start())
        f2(h, 0).start()

    for d in range(1, REACH + 1):

        @pl.when(jnp.logical_not(gets(d)))
        def _():
            for s in range(4):
                for h in range(hps):
                    win[s, h, d] = jnp.zeros(win.shape[3:], BF16)

    for h in range(hps):
        win[0, h, 0] = kv_ref[h]

    shift = heads.bit_length() - 1
    place = me * tok + lax.shift_right_logical(
        lax.broadcasted_iota(jnp.int32, (rows, 128), 0), shift
    )

    def scan(c, best):
        entry = starts_ref[pl.ds(c, 1), :]
        return jnp.maximum(best, jnp.where(entry <= place, entry, 0))

    best = lax.fori_loop(0, starts_ref.shape[0], scan, jnp.zeros((rows, 128), jnp.int32))
    start = jnp.max(jnp.transpose(best.astype(F32)), axis=0, keepdims=True).astype(jnp.int32)
    own = me * tok + lax.shift_right_logical(
        lax.broadcasted_iota(jnp.int32, (tok, rows), 1), shift
    )
    for d in range(REACH + 1):
        key = (me - d) * tok + lax.broadcasted_iota(jnp.int32, (tok, rows), 0)
        bias[d * tok:(d + 1) * tok, :] = jnp.where((key >= start) & (key <= own), 0.0, NEG)

    def compute(s, h):
        g = peer[s] * hps + h
        keys = win[s, h, :, 0].reshape(span, dim)
        values = win[s, h, :, 1].reshape(span, dim)
        keys_t = keys.T
        dk = jnp.zeros((span, dim), F32)
        dv = jnp.zeros((span, dim), F32)
        for r in range(0, rows, chunk):
            q = q_ref[g, r:r + chunk, :]
            do = do_ref[g, r:r + chunk, :]
            logits = dot_nt(keys, q) * (scaling * math.log2(math.e)) + bias[:, r:r + chunk]
            grad_prob = dot_nt(values, do)
            w = jnp.exp2(logits - jnp.max(logits, axis=0, keepdims=True))
            inv = 1.0 / jnp.sum(w, axis=0, keepdims=True)
            delta = jnp.sum(w * grad_prob, axis=0, keepdims=True) * inv
            probs = w * inv
            grad_logit = (probs * (grad_prob - delta)).astype(BF16)
            dv += dot(probs.astype(BF16), do)
            dk += dot(grad_logit, q)
            dq_t = dot(keys_t, grad_logit) * scaling
            dq_ref[g, r:r + chunk, :] = dq_t.T.astype(BF16)
        dk = (dk * scaling).reshape(REACH + 1, tok, dim)
        dv = dv.reshape(REACH + 1, tok, dim)
        if s == 0:
            p0[h, :, 0] = dk
            p0[h, :, 1] = dv
        elif s == 2:
            b3(h).wait_recv()
            pb[2, h, :, 0] = (dk + r3[h, :, 0].astype(F32)).astype(BF16)
            pb[2, h, :, 1] = (dv + r3[h, :, 1].astype(F32)).astype(BF16)
        else:
            pb[s, h, :, 0] = dk.astype(BF16)
            pb[s, h, :, 1] = dv.astype(BF16)

    def spread(h):
        for d in range(1, REACH + 1):

            @pl.when(gets(d))
            def _():
                f1(h, d).wait_recv()
                f3(h, d).start()
                f2(h, d).start()

    def relay(h):
        for d in range(REACH + 1):

            def go():
                f3(h, d).wait_recv()
                f4(h, d).start()

            when_d(gets, d, go)

    def arrived(f, h):
        for d in range(REACH + 1):
            when_d(gets, d, lambda: f(h, d).wait_recv())

    for h in range(hps):
        spread(h)
        compute(0, h)
    relay(0)
    for h in range(hps):
        arrived(f2, h)
        compute(1, h)
        b1(h).start()
        if h == 0:
            for k in range(1, hps):
                relay(k)
    for h in range(hps):
        arrived(f4, h)
        compute(3, h)
        b3(h).start()
        compute(2, h)
        b2(h).start()

    for h in range(hps):
        b1(h).wait_recv()
        b2(h).wait_recv()
        for d in range(REACH, -1, -1):
            total = p0[h, d] + r1[h, d].astype(F32) + r2[h, d].astype(F32)
            if d == 0:
                p0[h, d] = total
            else:
                ts[h, d] = total.astype(BF16)
                pl.when(gets(d))(lambda: bf(h, d).start())

    for h in range(hps):
        for d in range(1, REACH + 1):

            @pl.when(gives(d))
            def _():
                bf(h, d).wait_recv()
                p0[h, 0] += fb[h, d].astype(F32)

        dkv_ref[h] = p0[h, 0].astype(BF16)

    for h in range(hps):
        b1(h).wait_send()
        b2(h).wait_send()
        b3(h).wait_send()
        for d in range(REACH + 1):

            def sent():
                f2(h, d).wait_send()
                f3(h, d).wait_send()
                f4(h, d).wait_send()
                if d:
                    bf(h, d).wait_send()

            when_d(gets, d, sent)
            if d:
                pl.when(gives(d))(lambda: f1(h, d).wait_send())


def per_device(n_cp, n_tp, queries, key_heads, value_heads, grad_out, doc_starts):
    tok, kvh, heads, dim = queries.shape
    hps = key_heads.shape[1]
    rows = tok * heads
    reach = REACH + 1
    q = queries.transpose(1, 0, 2, 3).reshape(kvh, rows, dim)
    do = grad_out.transpose(1, 0, 2, 3).reshape(kvh, rows, dim)
    kv = jnp.stack([key_heads.transpose(1, 0, 2), value_heads.transpose(1, 0, 2)], axis=1)
    starts = doc_starts.reshape(-1, 128)
    unit = (2, tok, dim)
    dma = pltpu.SemaphoreType.DMA
    vmem = pl.BlockSpec(memory_space=pltpu.VMEM)
    dq, dkv = pl.pallas_call(
        functools.partial(kernel, n_cp, n_tp, heads, rows // 2),
        out_shape=(
            jax.ShapeDtypeStruct((kvh, rows, dim), BF16),
            jax.ShapeDtypeStruct((hps,) + unit, BF16),
        ),
        in_specs=[vmem] * 4,
        out_specs=(vmem, vmem),
        scratch_shapes=[
            pltpu.VMEM((4, hps, reach) + unit, BF16),
            pltpu.VMEM((reach * tok, rows), F32),
            pltpu.VMEM((hps, reach) + unit, F32),
            pltpu.VMEM((4, hps, reach) + unit, BF16),
            pltpu.VMEM((hps, reach) + unit, BF16),
            pltpu.VMEM((hps, reach) + unit, BF16),
            pltpu.VMEM((hps, reach) + unit, BF16),
            pltpu.VMEM((hps, reach) + unit, BF16),
            pltpu.VMEM((hps, reach) + unit, BF16),
            dma((4, hps, reach)),
            dma((hps, reach)),
            dma((hps, reach)),
            dma((hps, reach)),
            dma((hps, reach)),
            dma((hps, reach)),
            dma((hps,)),
            dma((hps,)),
            dma((hps,)),
            dma((hps,)),
            dma((hps,)),
            dma((hps,)),
            dma((hps, reach)),
        ],
        compiler_params=pltpu.CompilerParams(
            collective_id=0, has_side_effects=True, vmem_limit_bytes=56 * 1024 * 1024
        ),
    )(q, do, kv, starts)
    return (
        dq.reshape(kvh, tok, heads, dim).transpose(1, 0, 2, 3),
        dkv[:, 0].transpose(1, 0, 2),
        dkv[:, 1].transpose(1, 0, 2),
    )


def solution(mesh):
    placed = (
        P("cp", None, "tp", None),
        P("cp", "tp", None),
        P("cp", "tp", None),
        P("cp", None, "tp", None),
        P(),
    )
    return jax.shard_map(
        functools.partial(per_device, mesh.shape["cp"], mesh.shape["tp"]),
        mesh=mesh,
        in_specs=placed,
        out_specs=(P("cp", None, "tp", None), P("cp", "tp", None), P("cp", "tp", None)),
        check_vma=False,
    )
```

```python
import functools
import math

import jax
import jax.numpy as jnp
from jax import lax
from jax.experimental import pallas as pl
from jax.experimental.pallas import tpu as pltpu
from jax.sharding import PartitionSpec as P

REACH = 3
FIRST_DOC = 384
NEG = -1e30
MESH = pl.DeviceIdType.MESH
F32 = jnp.float32
BF16 = jnp.bfloat16
NT = (((1,), (1,)), ((), ()))


def dot(a, b):
    return jnp.dot(a, b, preferred_element_type=F32)


def dot_nt(a, b):
    return lax.dot_general(a, b, NT, preferred_element_type=F32)


def kernel(
    n_cp, n_tp, heads, chunk,
    q_hbm, do_hbm, k_ref, v_ref, starts_ref,
    dq_hbm, dk_ref, dv_ref,
    qs, dos, dqs, win, bias, p0, pb, r1, r2, r3, ts, fb,
    rs_w, rs_f, ss_1, ss_2, ss_3, ss_4, rs_1, rs_2, rs_3, sb_1, sb_2, sb_3, sb_f,
    sem_q, sem_do, sem_dq,
):
    me = lax.axis_index("cp")
    t = lax.axis_index("tp")
    tok, hps, dim = k_ref.shape
    rows = tok * heads
    span = (REACH + 1) * tok
    lead = FIRST_DOC // tok
    scaling = dim ** (-0.5)
    peer = (t, t + 1 - 2 * (t % 2), (t + n_tp // 2) % n_tp, n_tp - 1 - t)

    def sees(i, d):
        return (i - d >= 0) & ((i < lead) | (i - d >= lead))

    def gets(d):
        return sees(me, d)

    def gives(d):
        return (me + d < n_cp) & sees(me + d, d)

    def copy(src, dst, send, recv, where):
        return pltpu.make_async_remote_copy(
            src_ref=src, dst_ref=dst, send_sem=send, recv_sem=recv,
            device_id=where, device_id_type=MESH,
        )

    def to_cp(i):
        return {"cp": i}

    def to_tp(s):
        return {"tp": peer[s]}

    def f1(h, d):
        return copy(win.at[0, h, 0], win.at[0, h, d], ss_1.at[h, d], rs_w.at[0, h, d], to_cp(me + d))

    def f2(h, d):
        return copy(win.at[0, h, d], win.at[1, h, d], ss_2.at[h, d], rs_w.at[1, h, d], to_tp(1))

    def f3(h, d):
        return copy(win.at[0, h, d], win.at[2, h, d], ss_3.at[h, d], rs_w.at[2, h, d], to_tp(2))

    def f4(h, d):
        return copy(win.at[2, h, d], win.at[3, h, d], ss_4.at[h, d], rs_w.at[3, h, d], to_tp(1))

    def b1(h):
        return copy(pb.at[1, h], r1.at[h], sb_1.at[h], rs_1.at[h], to_tp(1))

    def b2(h, d):
        return copy(pb.at[2, h, d], r2.at[h, d], sb_2.at[h, d], rs_2.at[h, d], to_tp(2))

    def b3(h):
        return copy(pb.at[3, h], r3.at[h], sb_3.at[h], rs_3.at[h], to_tp(1))

    def bf(h, d):
        return copy(ts.at[h, d], fb.at[h, d], sb_f.at[h, d], rs_f.at[h, d], to_cp(me - d))

    def when_d(cond, d, action):
        if d == 0:
            action()
        else:
            pl.when(cond(d))(action)

    def local(array, scratch, sem, s, h):
        return pltpu.make_async_copy(
            array.at[:, peer[s] * hps + h], scratch.at[s, h], sem.at[s, h]
        )

    def fetch_q(s, h):
        return local(q_hbm, qs, sem_q, s, h)

    def fetch_do(s, h):
        return local(do_hbm, dos, sem_do, s, h)

    def put_dq(s, h):
        return pltpu.make_async_copy(
            dqs.at[s, h], dq_hbm.at[:, peer[s] * hps + h], sem_dq.at[s, h]
        )

    barrier = pltpu.get_barrier_semaphore()
    for s in (1, 2):
        pl.semaphore_signal(barrier, inc=1, device_id=to_tp(s), device_id_type=MESH)
    count = jnp.int32(2)
    for d in range(1, REACH + 1):
        count += gets(d).astype(jnp.int32) + gives(d).astype(jnp.int32)

        @pl.when(gets(d))
        def _():
            pl.semaphore_signal(barrier, inc=1, device_id=to_cp(me - d), device_id_type=MESH)

        @pl.when(gives(d))
        def _():
            pl.semaphore_signal(barrier, inc=1, device_id=to_cp(me + d), device_id_type=MESH)

    for h in range(hps):
        win[0, h, 0, 0] = k_ref[:, h, :]
        win[0, h, 0, 1] = v_ref[:, h, :]

    pl.semaphore_wait(barrier, count)

    for h in range(hps):
        f3(h, 0).start()
        for d in range(1, REACH + 1):
            pl.when(gives(d))(lambda: f1(h, d).start())
        f2(h, 0).start()

    for d in range(1, REACH + 1):

        @pl.when(jnp.logical_not(gets(d)))
        def _():
            for s in range(4):
                for h in range(hps):
                    win[s, h, d] = jnp.zeros(win.shape[3:], BF16)

    for s in (0, 3, 2, 1):
        for h in range(hps):
            fetch_q(s, h).start()
            fetch_do(s, h).start()

    shift = heads.bit_length() - 1
    place = me * tok + lax.shift_right_logical(
        lax.broadcasted_iota(jnp.int32, (rows, 128), 0), shift
    )

    def scan(c, best):
        entry = starts_ref[pl.ds(c, 1), :]
        return jnp.maximum(best, jnp.where(entry <= place, entry, 0))

    best = lax.fori_loop(0, starts_ref.shape[0], scan, jnp.zeros((rows, 128), jnp.int32))
    start = jnp.max(jnp.transpose(best.astype(F32)), axis=0, keepdims=True).astype(jnp.int32)
    own = me * tok + lax.shift_right_logical(
        lax.broadcasted_iota(jnp.int32, (tok, rows), 1), shift
    )
    for d in range(REACH + 1):
        key = (me - d) * tok + lax.broadcasted_iota(jnp.int32, (tok, rows), 0)
        bias[d * tok:(d + 1) * tok, :] = jnp.where((key >= start) & (key <= own), 0.0, NEG)

    def compute(s, h):
        fetch_q(s, h).wait()
        fetch_do(s, h).wait()
        q_all = qs[s, h].reshape(rows, dim)
        do_all = dos[s, h].reshape(rows, dim)
        keys = win[s, h, :, 0].reshape(span, dim)
        values = win[s, h, :, 1].reshape(span, dim)
        keys_t = keys.T
        dk = jnp.zeros((span, dim), F32)
        dv = jnp.zeros((span, dim), F32)
        for r in range(0, rows, chunk):
            q = q_all[r:r + chunk]
            do = do_all[r:r + chunk]
            logits = dot_nt(keys, q) * (scaling * math.log2(math.e)) + bias[:, r:r + chunk]
            grad_prob = dot_nt(values, do)
            w = jnp.exp2(logits - jnp.max(logits, axis=0, keepdims=True))
            inv = 1.0 / jnp.sum(w, axis=0, keepdims=True)
            delta = jnp.sum(w * grad_prob, axis=0, keepdims=True) * inv
            probs = w * inv
            grad_logit = (probs * (grad_prob - delta)).astype(BF16)
            dv += dot(probs.astype(BF16), do)
            dk += dot(grad_logit, q)
            dq_t = dot(keys_t, grad_logit) * scaling
            dqs[s, h, r // heads:(r + chunk) // heads] = (
                dq_t.T.astype(BF16).reshape(chunk // heads, heads, dim)
            )
        put_dq(s, h).start()
        dk = (dk * scaling).reshape(REACH + 1, tok, dim)
        dv = dv.reshape(REACH + 1, tok, dim)
        if s == 0:
            p0[h, :, 0] = dk
            p0[h, :, 1] = dv
        elif s == 2:
            b3(h).wait_recv()
            pb[2, h, :, 0] = (dk + r3[h, :, 0].astype(F32)).astype(BF16)
            pb[2, h, :, 1] = (dv + r3[h, :, 1].astype(F32)).astype(BF16)
        else:
            pb[s, h, :, 0] = dk.astype(BF16)
            pb[s, h, :, 1] = dv.astype(BF16)

    def spread(h):
        for d in range(1, REACH + 1):

            @pl.when(gets(d))
            def _():
                f1(h, d).wait_recv()
                f3(h, d).start()
                f2(h, d).start()

    def relay(h):
        for d in range(REACH + 1):

            def go():
                f3(h, d).wait_recv()
                f4(h, d).start()

            when_d(gets, d, go)

    def arrived(f, h):
        for d in range(REACH + 1):
            when_d(gets, d, lambda: f(h, d).wait_recv())

    def foreign(h):
        arrived(f4, h)
        compute(3, h)
        b3(h).start()
        compute(2, h)
        for d in range(REACH, -1, -1):
            when_d(gets, d, lambda: b2(h, d).start())

    def near(h):
        arrived(f2, h)
        compute(1, h)
        b1(h).start()

    def settle(h):
        b1(h).wait_recv()
        for d in range(REACH, -1, -1):

            def go():
                b2(h, d).wait_recv()
                total = p0[h, d] + r1[h, d].astype(F32) + r2[h, d].astype(F32)
                if d == 0:
                    p0[h, d] = total
                else:
                    ts[h, d] = total.astype(BF16)
                    bf(h, d).start()

            when_d(gets, d, go)

    for h in range(hps):
        spread(h)
        compute(0, h)
    for h in range(hps):
        relay(h)
        foreign(h)
        if h:
            settle(h - 1)
        near(h)
    settle(hps - 1)

    for h in range(hps):
        for d in range(REACH, 0, -1):

            @pl.when(gives(d))
            def _():
                bf(h, d).wait_recv()
                p0[h, 0] += fb[h, d].astype(F32)

        dk_ref[:, h, :] = p0[h, 0, 0].astype(BF16)
        dv_ref[:, h, :] = p0[h, 0, 1].astype(BF16)

    for h in range(hps):
        b1(h).wait_send()
        b3(h).wait_send()
        for s in range(4):
            put_dq(s, h).wait()
        for d in range(REACH + 1):

            def sent():
                f2(h, d).wait_send()
                f3(h, d).wait_send()
                f4(h, d).wait_send()
                b2(h, d).wait_send()
                if d:
                    bf(h, d).wait_send()

            when_d(gets, d, sent)
            if d:
                pl.when(gives(d))(lambda: f1(h, d).wait_send())


def per_device(n_cp, n_tp, queries, key_heads, value_heads, grad_out, doc_starts):
    tok, kvh, heads, dim = queries.shape
    hps = key_heads.shape[1]
    rows = tok * heads
    reach = REACH + 1
    starts = doc_starts.reshape(-1, 128)
    unit = (2, tok, dim)
    dma = pltpu.SemaphoreType.DMA
    vmem = pl.BlockSpec(memory_space=pltpu.VMEM)
    hbm = pl.BlockSpec(memory_space=pl.ANY)
    return pl.pallas_call(
        functools.partial(kernel, n_cp, n_tp, heads, rows // 2),
        out_shape=(
            jax.ShapeDtypeStruct(queries.shape, BF16),
            jax.ShapeDtypeStruct(key_heads.shape, BF16),
            jax.ShapeDtypeStruct(value_heads.shape, BF16),
        ),
        in_specs=[hbm, hbm, vmem, vmem, vmem],
        out_specs=(hbm, vmem, vmem),
        scratch_shapes=[
            pltpu.VMEM((4, hps, tok, heads, dim), BF16),
            pltpu.VMEM((4, hps, tok, heads, dim), BF16),
            pltpu.VMEM((4, hps, tok, heads, dim), BF16),
            pltpu.VMEM((4, hps, reach) + unit, BF16),
            pltpu.VMEM((reach * tok, rows), F32),
            pltpu.VMEM((hps, reach) + unit, F32),
            pltpu.VMEM((4, hps, reach) + unit, BF16),
            pltpu.VMEM((hps, reach) + unit, BF16),
            pltpu.VMEM((hps, reach) + unit, BF16),
            pltpu.VMEM((hps, reach) + unit, BF16),
            pltpu.VMEM((hps, reach) + unit, BF16),
            pltpu.VMEM((hps, reach) + unit, BF16),
            dma((4, hps, reach)),
            dma((hps, reach)),
            dma((hps, reach)),
            dma((hps, reach)),
            dma((hps, reach)),
            dma((hps, reach)),
            dma((hps,)),
            dma((hps, reach)),
            dma((hps,)),
            dma((hps,)),
            dma((hps, reach)),
            dma((hps,)),
            dma((hps, reach)),
            dma((4, hps)),
            dma((4, hps)),
            dma((4, hps)),
        ],
        compiler_params=pltpu.CompilerParams(
            collective_id=0, has_side_effects=True, vmem_limit_bytes=56 * 1024 * 1024
        ),
    )(queries, grad_out, key_heads, value_heads, starts)


def solution(mesh):
    placed = (
        P("cp", None, "tp", None),
        P("cp", "tp", None),
        P("cp", "tp", None),
        P("cp", None, "tp", None),
        P(),
    )
    return jax.shard_map(
        functools.partial(per_device, mesh.shape["cp"], mesh.shape["tp"]),
        mesh=mesh,
        in_specs=placed,
        out_specs=(P("cp", None, "tp", None), P("cp", "tp", None), P("cp", "tp", None)),
        check_vma=False,
    )
```

```python
import functools
import math

import jax
import jax.numpy as jnp
from jax import lax
from jax.experimental import pallas as pl
from jax.experimental.pallas import tpu as pltpu
from jax.sharding import PartitionSpec as P

REACH = 3
FIRST_DOC = 384
NEG = -1e30
MESH = pl.DeviceIdType.MESH
F32 = jnp.float32
BF16 = jnp.bfloat16
NT = (((1,), (1,)), ((), ()))


def dot(a, b):
    return jnp.dot(a, b, preferred_element_type=F32)


def dot_nt(a, b):
    return lax.dot_general(a, b, NT, preferred_element_type=F32)


def kernel(
    n_cp, n_tp, heads, chunk,
    q_hbm, do_hbm, k_ref, v_ref, starts_ref,
    dq_hbm, dk_ref, dv_ref,
    qs, dos, dqs, win, bias, p0, pb, r1, r2, r3, ts, fb,
    rs_w, rs_f, ss_1, ss_2, ss_3, ss_4, rs_1, rs_2, rs_3, sb_1, sb_2, sb_3, sb_f,
    sem_q, sem_do, sem_dq,
):
    me = lax.axis_index("cp")
    t = lax.axis_index("tp")
    tok, hps, dim = k_ref.shape
    rows = tok * heads
    span = (REACH + 1) * tok
    lead = FIRST_DOC // tok
    scaling = dim ** (-0.5)
    peer = (t, t + 1 - 2 * (t % 2), (t + n_tp // 2) % n_tp, n_tp - 1 - t)

    def sees(i, d):
        return (i - d >= 0) & ((i < lead) | (i - d >= lead))

    def gets(d):
        return sees(me, d)

    def gives(d):
        return (me + d < n_cp) & sees(me + d, d)

    def copy(src, dst, send, recv, where):
        return pltpu.make_async_remote_copy(
            src_ref=src, dst_ref=dst, send_sem=send, recv_sem=recv,
            device_id=where, device_id_type=MESH,
        )

    def to_cp(i):
        return {"cp": i}

    def to_tp(s):
        return {"tp": peer[s]}

    def f1(h, d):
        return copy(win.at[0, h, 0], win.at[0, h, d], ss_1.at[h, d], rs_w.at[0, h, d], to_cp(me + d))

    def f2(h, d):
        return copy(win.at[0, h, d], win.at[1, h, d], ss_2.at[h, d], rs_w.at[1, h, d], to_tp(1))

    def f3(h, d):
        return copy(win.at[0, h, d], win.at[2, h, d], ss_3.at[h, d], rs_w.at[2, h, d], to_tp(2))

    def f4(h, d):
        return copy(win.at[2, h, d], win.at[3, h, d], ss_4.at[h, d], rs_w.at[3, h, d], to_tp(1))

    def b1(h):
        return copy(pb.at[1, h], r1.at[h], sb_1.at[h], rs_1.at[h], to_tp(1))

    def b2(h, d):
        return copy(pb.at[2, h, d], r2.at[h, d], sb_2.at[h, d], rs_2.at[h, d], to_tp(2))

    def b3(h):
        return copy(pb.at[3, h], r3.at[h], sb_3.at[h], rs_3.at[h], to_tp(1))

    def bf(h, d):
        return copy(ts.at[h, d], fb.at[h, d], sb_f.at[h, d], rs_f.at[h, d], to_cp(me - d))

    def when_d(cond, d, action):
        if d == 0:
            action()
        else:
            pl.when(cond(d))(action)

    def local(array, scratch, sem, s, h):
        return pltpu.make_async_copy(
            array.at[:, peer[s] * hps + h], scratch.at[s, h], sem.at[s, h]
        )

    def fetch_q(s, h):
        return local(q_hbm, qs, sem_q, s, h)

    def fetch_do(s, h):
        return local(do_hbm, dos, sem_do, s, h)

    def put_dq(s, h):
        return pltpu.make_async_copy(
            dqs.at[s, h], dq_hbm.at[:, peer[s] * hps + h], sem_dq.at[s, h]
        )

    barrier = pltpu.get_barrier_semaphore()
    for s in (1, 2):
        pl.semaphore_signal(barrier, inc=1, device_id=to_tp(s), device_id_type=MESH)
    count = jnp.int32(2)
    for d in range(1, REACH + 1):
        count += gets(d).astype(jnp.int32) + gives(d).astype(jnp.int32)

        @pl.when(gets(d))
        def _():
            pl.semaphore_signal(barrier, inc=1, device_id=to_cp(me - d), device_id_type=MESH)

        @pl.when(gives(d))
        def _():
            pl.semaphore_signal(barrier, inc=1, device_id=to_cp(me + d), device_id_type=MESH)

    for h in range(hps):
        win[0, h, 0, 0] = k_ref[:, h, :]
        win[0, h, 0, 1] = v_ref[:, h, :]

    pl.semaphore_wait(barrier, count)

    for h in range(hps):
        f3(h, 0).start()
        for d in range(1, REACH + 1):
            pl.when(gives(d))(lambda: f1(h, d).start())
        f2(h, 0).start()

    for d in range(1, REACH + 1):

        @pl.when(jnp.logical_not(gets(d)))
        def _():
            for s in range(4):
                for h in range(hps):
                    win[s, h, d] = jnp.zeros(win.shape[3:], BF16)

    for s in (0, 3, 2, 1):
        for h in range(hps):
            fetch_q(s, h).start()
            fetch_do(s, h).start()

    shift = heads.bit_length() - 1
    place = me * tok + lax.shift_right_logical(
        lax.broadcasted_iota(jnp.int32, (rows, 128), 0), shift
    )

    def scan(c, best):
        entry = starts_ref[pl.ds(c, 1), :]
        return jnp.maximum(best, jnp.where(entry <= place, entry, 0))

    best = lax.fori_loop(0, starts_ref.shape[0], scan, jnp.zeros((rows, 128), jnp.int32))
    start = jnp.max(jnp.transpose(best.astype(F32)), axis=0, keepdims=True).astype(jnp.int32)
    own = me * tok + lax.shift_right_logical(
        lax.broadcasted_iota(jnp.int32, (tok, rows), 1), shift
    )
    for d in range(REACH + 1):
        key = (me - d) * tok + lax.broadcasted_iota(jnp.int32, (tok, rows), 0)
        bias[d * tok:(d + 1) * tok, :] = jnp.where((key >= start) & (key <= own), 0.0, NEG)

    def compute(s, h):
        fetch_q(s, h).wait()
        fetch_do(s, h).wait()
        q_all = qs[s, h].reshape(rows, dim)
        do_all = dos[s, h].reshape(rows, dim)
        keys = win[s, h, :, 0].reshape(span, dim)
        values = win[s, h, :, 1].reshape(span, dim)
        keys_t = keys.T
        dk = jnp.zeros((span, dim), F32)
        dv = jnp.zeros((span, dim), F32)
        for r in range(0, rows, chunk):
            q = q_all[r:r + chunk]
            do = do_all[r:r + chunk]
            logits = dot_nt(keys, q) * (scaling * math.log2(math.e)) + bias[:, r:r + chunk]
            grad_prob = dot_nt(values, do)
            w = jnp.exp2(logits - jnp.max(logits, axis=0, keepdims=True))
            inv = 1.0 / jnp.sum(w, axis=0, keepdims=True)
            delta = jnp.sum(w * grad_prob, axis=0, keepdims=True) * inv
            probs = w * inv
            grad_logit = (probs * (grad_prob - delta)).astype(BF16)
            dv += dot(probs.astype(BF16), do)
            dk += dot(grad_logit, q)
            dq_t = dot(keys_t, grad_logit) * scaling
            dqs[s, h, r // heads:(r + chunk) // heads] = (
                dq_t.T.astype(BF16).reshape(chunk // heads, heads, dim)
            )
        put_dq(s, h).start()
        dk = (dk * scaling).reshape(REACH + 1, tok, dim)
        dv = dv.reshape(REACH + 1, tok, dim)
        if s == 0:
            p0[h, :, 0] = dk
            p0[h, :, 1] = dv
        elif s == 2:
            b3(h).wait_recv()
            pb[2, h, :, 0] = (dk + r3[h, :, 0].astype(F32)).astype(BF16)
            pb[2, h, :, 1] = (dv + r3[h, :, 1].astype(F32)).astype(BF16)
        else:
            pb[s, h, :, 0] = dk.astype(BF16)
            pb[s, h, :, 1] = dv.astype(BF16)

    def spread(h):
        for d in range(1, REACH + 1):

            @pl.when(gets(d))
            def _():
                f1(h, d).wait_recv()
                f3(h, d).start()
                f2(h, d).start()

    def relay(h):
        for d in range(REACH + 1):

            def go():
                f3(h, d).wait_recv()
                f4(h, d).start()

            when_d(gets, d, go)

    def arrived(f, h):
        for d in range(REACH + 1):
            when_d(gets, d, lambda: f(h, d).wait_recv())

    def foreign(h):
        arrived(f4, h)
        compute(3, h)
        b3(h).start()
        compute(2, h)
        for d in range(REACH, -1, -1):
            when_d(gets, d, lambda: b2(h, d).start())

    def near(h):
        arrived(f2, h)
        compute(1, h)
        b1(h).start()

    def settle(h):
        b1(h).wait_recv()
        for d in range(REACH, -1, -1):

            def go():
                b2(h, d).wait_recv()
                total = p0[h, d] + r1[h, d].astype(F32) + r2[h, d].astype(F32)
                if d == 0:
                    p0[h, d] = total
                else:
                    ts[h, d] = total.astype(BF16)
                    bf(h, d).start()

            when_d(gets, d, go)

    for h in range(hps):
        spread(h)
        compute(0, h)
    for h in range(hps):
        relay(h)
        foreign(h)
        if h:
            settle(h - 1)
        near(h)
    settle(hps - 1)

    for h in range(hps):
        for d in range(REACH, 0, -1):

            @pl.when(gives(d))
            def _():
                bf(h, d).wait_recv()
                p0[h, 0] += fb[h, d].astype(F32)

        dk_ref[:, h, :] = p0[h, 0, 0].astype(BF16)
        dv_ref[:, h, :] = p0[h, 0, 1].astype(BF16)

    for h in range(hps):
        b1(h).wait_send()
        b3(h).wait_send()
        for s in range(4):
            put_dq(s, h).wait()
        for d in range(REACH + 1):

            def sent():
                f2(h, d).wait_send()
                f3(h, d).wait_send()
                f4(h, d).wait_send()
                b2(h, d).wait_send()
                if d:
                    bf(h, d).wait_send()

            when_d(gets, d, sent)
            if d:
                pl.when(gives(d))(lambda: f1(h, d).wait_send())


def write_out(dq_in, dk_in, dv_in, dq_out, dk_out, dv_out, sems):
    copies = [
        pltpu.make_async_copy(src, dst, sems.at[k])
        for k, (src, dst) in enumerate(((dq_in, dq_out), (dk_in, dk_out), (dv_in, dv_out)))
    ]
    for copy in copies:
        copy.start()
    for copy in copies:
        copy.wait()


def per_device(n_cp, n_tp, queries, key_heads, value_heads, grad_out, doc_starts):
    tok, kvh, heads, dim = queries.shape
    hps = key_heads.shape[1]
    rows = tok * heads
    reach = REACH + 1
    starts = doc_starts.reshape(-1, 128)
    unit = (2, tok, dim)
    dma = pltpu.SemaphoreType.DMA
    vmem = pl.BlockSpec(memory_space=pltpu.VMEM)
    hbm = pl.BlockSpec(memory_space=pl.ANY)
    queries = pltpu.with_memory_space_constraint(queries, pltpu.HBM)
    grad_out = pltpu.with_memory_space_constraint(grad_out, pltpu.HBM)
    grads = pl.pallas_call(
        functools.partial(kernel, n_cp, n_tp, heads, rows),
        out_shape=(
            jax.ShapeDtypeStruct(queries.shape, BF16),
            jax.ShapeDtypeStruct(key_heads.shape, BF16),
            jax.ShapeDtypeStruct(value_heads.shape, BF16),
        ),
        in_specs=[hbm, hbm, vmem, vmem, vmem],
        out_specs=(hbm, vmem, vmem),
        scratch_shapes=[
            pltpu.VMEM((4, hps, tok, heads, dim), BF16),
            pltpu.VMEM((4, hps, tok, heads, dim), BF16),
            pltpu.VMEM((4, hps, tok, heads, dim), BF16),
            pltpu.VMEM((4, hps, reach) + unit, BF16),
            pltpu.VMEM((reach * tok, rows), F32),
            pltpu.VMEM((hps, reach) + unit, F32),
            pltpu.VMEM((4, hps, reach) + unit, BF16),
            pltpu.VMEM((hps, reach) + unit, BF16),
            pltpu.VMEM((hps, reach) + unit, BF16),
            pltpu.VMEM((hps, reach) + unit, BF16),
            pltpu.VMEM((hps, reach) + unit, BF16),
            pltpu.VMEM((hps, reach) + unit, BF16),
            dma((4, hps, reach)),
            dma((hps, reach)),
            dma((hps, reach)),
            dma((hps, reach)),
            dma((hps, reach)),
            dma((hps, reach)),
            dma((hps,)),
            dma((hps, reach)),
            dma((hps,)),
            dma((hps,)),
            dma((hps, reach)),
            dma((hps,)),
            dma((hps, reach)),
            dma((4, hps)),
            dma((4, hps)),
            dma((4, hps)),
        ],
        compiler_params=pltpu.CompilerParams(
            collective_id=0, has_side_effects=True, vmem_limit_bytes=24 * 1024 * 1024
        ),
    )(queries, grad_out, key_heads, value_heads, starts)
    return pl.pallas_call(
        write_out,
        out_shape=tuple(jax.ShapeDtypeStruct(g.shape, g.dtype) for g in grads),
        in_specs=[vmem] * 3,
        out_specs=(hbm, hbm, hbm),
        scratch_shapes=[dma((3,))],
        compiler_params=pltpu.CompilerParams(vmem_limit_bytes=24 * 1024 * 1024),
    )(*grads)


def solution(mesh):
    placed = (
        P("cp", None, "tp", None),
        P("cp", "tp", None),
        P("cp", "tp", None),
        P("cp", None, "tp", None),
        P(),
    )
    return jax.shard_map(
        functools.partial(per_device, mesh.shape["cp"], mesh.shape["tp"]),
        mesh=mesh,
        in_specs=placed,
        out_specs=(P("cp", None, "tp", None), P("cp", "tp", None), P("cp", "tp", None)),
        check_vma=False,
    )
```

```python
import functools
import math

import jax
import jax.numpy as jnp
from jax import lax
from jax.experimental import pallas as pl
from jax.experimental.pallas import tpu as pltpu
from jax.sharding import PartitionSpec as P

REACH = 3
FIRST_DOC = 384
NEG = -1e30
MESH = pl.DeviceIdType.MESH
F32 = jnp.float32
BF16 = jnp.bfloat16
NT = (((1,), (1,)), ((), ()))


def dot(a, b):
    return jnp.dot(a, b, preferred_element_type=F32)


def dot_nt(a, b):
    return lax.dot_general(a, b, NT, preferred_element_type=F32)


def kernel(
    n_cp, n_tp, heads, chunk,
    q_hbm, do_hbm, k_hbm, v_hbm, starts_hbm,
    dq_hbm, dk_ref, dv_ref,
    k_ref, v_ref, starts_ref, qs, dos, dqs, win, bias, p0, pb, r1, r2, r3, ts, fb,
    rs_w, rs_f, ss_1, ss_2, ss_3, ss_4, rs_1, rs_2, rs_3, sb_1, sb_2, sb_3, sb_f,
    sem_in, sem_q, sem_do, sem_dq,
):
    me = lax.axis_index("cp")
    t = lax.axis_index("tp")
    tok, hps, dim = k_ref.shape
    rows = tok * heads
    span = (REACH + 1) * tok
    lead = FIRST_DOC // tok
    scaling = dim ** (-0.5)
    peer = (t, t + 1 - 2 * (t % 2), (t + n_tp // 2) % n_tp, n_tp - 1 - t)

    def sees(i, d):
        return (i - d >= 0) & ((i < lead) | (i - d >= lead))

    def gets(d):
        return sees(me, d)

    def gives(d):
        return (me + d < n_cp) & sees(me + d, d)

    def copy(src, dst, send, recv, where):
        return pltpu.make_async_remote_copy(
            src_ref=src, dst_ref=dst, send_sem=send, recv_sem=recv,
            device_id=where, device_id_type=MESH,
        )

    def to_cp(i):
        return {"cp": i}

    def to_tp(s):
        return {"tp": peer[s]}

    def f1(h, d):
        return copy(win.at[0, h, 0], win.at[0, h, d], ss_1.at[h, d], rs_w.at[0, h, d], to_cp(me + d))

    def f2(h, d):
        return copy(win.at[0, h, d], win.at[1, h, d], ss_2.at[h, d], rs_w.at[1, h, d], to_tp(1))

    def f3(h, d):
        return copy(win.at[0, h, d], win.at[2, h, d], ss_3.at[h, d], rs_w.at[2, h, d], to_tp(2))

    def f4(h, d):
        return copy(win.at[2, h, d], win.at[3, h, d], ss_4.at[h, d], rs_w.at[3, h, d], to_tp(1))

    def b1(h):
        return copy(pb.at[1, h], r1.at[h], sb_1.at[h], rs_1.at[h], to_tp(1))

    def b2(h, d):
        return copy(pb.at[2, h, d], r2.at[h, d], sb_2.at[h, d], rs_2.at[h, d], to_tp(2))

    def b3(h):
        return copy(pb.at[3, h], r3.at[h], sb_3.at[h], rs_3.at[h], to_tp(1))

    def bf(h, d):
        return copy(ts.at[h, d], fb.at[h, d], sb_f.at[h, d], rs_f.at[h, d], to_cp(me - d))

    def when_d(cond, d, action):
        if d == 0:
            action()
        else:
            pl.when(cond(d))(action)

    def local(array, scratch, sem, s, h):
        return pltpu.make_async_copy(
            array.at[:, peer[s] * hps + h], scratch.at[s, h], sem.at[s, h]
        )

    def fetch_q(s, h):
        return local(q_hbm, qs, sem_q, s, h)

    def fetch_do(s, h):
        return local(do_hbm, dos, sem_do, s, h)

    def put_dq(s, h):
        return pltpu.make_async_copy(
            dqs.at[s, h], dq_hbm.at[:, peer[s] * hps + h], sem_dq.at[s, h]
        )

    fetches = [
        pltpu.make_async_copy(src, dst, sem_in.at[k])
        for k, (src, dst) in enumerate(
            ((k_hbm, k_ref), (v_hbm, v_ref), (starts_hbm, starts_ref))
        )
    ]
    for fetch in fetches:
        fetch.start()

    barrier = pltpu.get_barrier_semaphore()
    for s in (1, 2):
        pl.semaphore_signal(barrier, inc=1, device_id=to_tp(s), device_id_type=MESH)
    count = jnp.int32(2)
    for d in range(1, REACH + 1):
        count += gets(d).astype(jnp.int32) + gives(d).astype(jnp.int32)

        @pl.when(gets(d))
        def _():
            pl.semaphore_signal(barrier, inc=1, device_id=to_cp(me - d), device_id_type=MESH)

        @pl.when(gives(d))
        def _():
            pl.semaphore_signal(barrier, inc=1, device_id=to_cp(me + d), device_id_type=MESH)

    fetches[0].wait()
    fetches[1].wait()
    for h in range(hps):
        win[0, h, 0, 0] = k_ref[:, h, :]
        win[0, h, 0, 1] = v_ref[:, h, :]

    pl.semaphore_wait(barrier, count)

    for h in range(hps):
        f3(h, 0).start()
        for d in range(1, REACH + 1):
            pl.when(gives(d))(lambda: f1(h, d).start())
        f2(h, 0).start()

    for d in range(1, REACH + 1):

        @pl.when(jnp.logical_not(gets(d)))
        def _():
            for s in range(4):
                for h in range(hps):
                    win[s, h, d] = jnp.zeros(win.shape[3:], BF16)

    for s in (0, 3, 2, 1):
        for h in range(hps):
            fetch_q(s, h).start()
            fetch_do(s, h).start()

    fetches[2].wait()
    shift = heads.bit_length() - 1
    place = me * tok + lax.shift_right_logical(
        lax.broadcasted_iota(jnp.int32, (rows, 128), 0), shift
    )

    def scan(c, best):
        entry = starts_ref[pl.ds(c, 1), :]
        return jnp.maximum(best, jnp.where(entry <= place, entry, 0))

    best = lax.fori_loop(0, starts_ref.shape[0], scan, jnp.zeros((rows, 128), jnp.int32))
    start = jnp.max(jnp.transpose(best.astype(F32)), axis=0, keepdims=True).astype(jnp.int32)
    own = me * tok + lax.shift_right_logical(
        lax.broadcasted_iota(jnp.int32, (tok, rows), 1), shift
    )
    for d in range(REACH + 1):
        key = (me - d) * tok + lax.broadcasted_iota(jnp.int32, (tok, rows), 0)
        bias[d * tok:(d + 1) * tok, :] = jnp.where((key >= start) & (key <= own), 0.0, NEG)

    def compute(s, h):
        fetch_q(s, h).wait()
        fetch_do(s, h).wait()
        q_all = qs[s, h].reshape(rows, dim)
        do_all = dos[s, h].reshape(rows, dim)
        keys = win[s, h, :, 0].reshape(span, dim)
        values = win[s, h, :, 1].reshape(span, dim)
        keys_t = keys.T
        dk = jnp.zeros((span, dim), F32)
        dv = jnp.zeros((span, dim), F32)
        for r in range(0, rows, chunk):
            q = q_all[r:r + chunk]
            do = do_all[r:r + chunk]
            logits = dot_nt(keys, q) * (scaling * math.log2(math.e)) + bias[:, r:r + chunk]
            grad_prob = dot_nt(values, do)
            w = jnp.exp2(logits - jnp.max(logits, axis=0, keepdims=True))
            inv = 1.0 / jnp.sum(w, axis=0, keepdims=True)
            delta = jnp.sum(w * grad_prob, axis=0, keepdims=True) * inv
            probs = w * inv
            grad_logit = (probs * (grad_prob - delta)).astype(BF16)
            dv += dot(probs.astype(BF16), do)
            dk += dot(grad_logit, q)
            dq_t = dot(keys_t, grad_logit) * scaling
            dqs[s, h, r // heads:(r + chunk) // heads] = (
                dq_t.T.astype(BF16).reshape(chunk // heads, heads, dim)
            )
        put_dq(s, h).start()
        dk = (dk * scaling).reshape(REACH + 1, tok, dim)
        dv = dv.reshape(REACH + 1, tok, dim)
        if s == 0:
            p0[h, :, 0] = dk
            p0[h, :, 1] = dv
        elif s == 2:
            b3(h).wait_recv()
            pb[2, h, :, 0] = (dk + r3[h, :, 0].astype(F32)).astype(BF16)
            pb[2, h, :, 1] = (dv + r3[h, :, 1].astype(F32)).astype(BF16)
        else:
            pb[s, h, :, 0] = dk.astype(BF16)
            pb[s, h, :, 1] = dv.astype(BF16)

    def spread(h):
        for d in range(1, REACH + 1):

            @pl.when(gets(d))
            def _():
                f1(h, d).wait_recv()
                f3(h, d).start()
                f2(h, d).start()

    def relay(h):
        for d in range(REACH + 1):

            def go():
                f3(h, d).wait_recv()
                f4(h, d).start()

            when_d(gets, d, go)

    def arrived(f, h):
        for d in range(REACH + 1):
            when_d(gets, d, lambda: f(h, d).wait_recv())

    def foreign(h):
        arrived(f4, h)
        compute(3, h)
        b3(h).start()
        compute(2, h)
        for d in range(REACH, -1, -1):
            when_d(gets, d, lambda: b2(h, d).start())

    def near(h):
        arrived(f2, h)
        compute(1, h)
        b1(h).start()

    def settle(h):
        b1(h).wait_recv()
        for d in range(REACH, -1, -1):

            def go():
                b2(h, d).wait_recv()
                total = p0[h, d] + r1[h, d].astype(F32) + r2[h, d].astype(F32)
                if d == 0:
                    p0[h, d] = total
                else:
                    ts[h, d] = total.astype(BF16)
                    bf(h, d).start()

            when_d(gets, d, go)

    for h in range(hps):
        spread(h)
        compute(0, h)
    for h in range(hps):
        relay(h)
        foreign(h)
        if h:
            settle(h - 1)
        near(h)
    settle(hps - 1)

    for h in range(hps):
        for d in range(REACH, 0, -1):

            @pl.when(gives(d))
            def _():
                bf(h, d).wait_recv()
                p0[h, 0] += fb[h, d].astype(F32)

        dk_ref[:, h, :] = p0[h, 0, 0].astype(BF16)
        dv_ref[:, h, :] = p0[h, 0, 1].astype(BF16)

    for h in range(hps):
        b1(h).wait_send()
        b3(h).wait_send()
        for s in range(4):
            put_dq(s, h).wait()
        for d in range(REACH + 1):

            def sent():
                f2(h, d).wait_send()
                f3(h, d).wait_send()
                f4(h, d).wait_send()
                b2(h, d).wait_send()
                if d:
                    bf(h, d).wait_send()

            when_d(gets, d, sent)
            if d:
                pl.when(gives(d))(lambda: f1(h, d).wait_send())


def write_out(dq_in, dk_in, dv_in, dq_out, dk_out, dv_out, sems):
    copies = [
        pltpu.make_async_copy(src, dst, sems.at[k])
        for k, (src, dst) in enumerate(((dq_in, dq_out), (dk_in, dk_out), (dv_in, dv_out)))
    ]
    for copy in copies:
        copy.start()
    for copy in copies:
        copy.wait()


def per_device(n_cp, n_tp, queries, key_heads, value_heads, grad_out, doc_starts):
    tok, kvh, heads, dim = queries.shape
    hps = key_heads.shape[1]
    rows = tok * heads
    reach = REACH + 1
    starts = doc_starts.reshape(-1, 128)
    unit = (2, tok, dim)
    dma = pltpu.SemaphoreType.DMA
    vmem = pl.BlockSpec(memory_space=pltpu.VMEM)
    hbm = pl.BlockSpec(memory_space=pl.ANY)
    operands = [
        pltpu.with_memory_space_constraint(a, pltpu.HBM)
        for a in (queries, grad_out, key_heads, value_heads, starts)
    ]
    grads = pl.pallas_call(
        functools.partial(kernel, n_cp, n_tp, heads, rows),
        out_shape=(
            jax.ShapeDtypeStruct(queries.shape, BF16),
            jax.ShapeDtypeStruct(key_heads.shape, BF16),
            jax.ShapeDtypeStruct(value_heads.shape, BF16),
        ),
        in_specs=[hbm] * 5,
        out_specs=(hbm, vmem, vmem),
        scratch_shapes=[
            pltpu.VMEM(key_heads.shape, BF16),
            pltpu.VMEM(value_heads.shape, BF16),
            pltpu.VMEM(starts.shape, jnp.int32),
            pltpu.VMEM((4, hps, tok, heads, dim), BF16),
            pltpu.VMEM((4, hps, tok, heads, dim), BF16),
            pltpu.VMEM((4, hps, tok, heads, dim), BF16),
            pltpu.VMEM((4, hps, reach) + unit, BF16),
            pltpu.VMEM((reach * tok, rows), F32),
            pltpu.VMEM((hps, reach) + unit, F32),
            pltpu.VMEM((4, hps, reach) + unit, BF16),
            pltpu.VMEM((hps, reach) + unit, BF16),
            pltpu.VMEM((hps, reach) + unit, BF16),
            pltpu.VMEM((hps, reach) + unit, BF16),
            pltpu.VMEM((hps, reach) + unit, BF16),
            pltpu.VMEM((hps, reach) + unit, BF16),
            dma((4, hps, reach)),
            dma((hps, reach)),
            dma((hps, reach)),
            dma((hps, reach)),
            dma((hps, reach)),
            dma((hps, reach)),
            dma((hps,)),
            dma((hps, reach)),
            dma((hps,)),
            dma((hps,)),
            dma((hps, reach)),
            dma((hps,)),
            dma((hps, reach)),
            dma((3,)),
            dma((4, hps)),
            dma((4, hps)),
            dma((4, hps)),
        ],
        compiler_params=pltpu.CompilerParams(
            collective_id=0, has_side_effects=True, vmem_limit_bytes=24 * 1024 * 1024
        ),
    )(*operands)
    return pl.pallas_call(
        write_out,
        out_shape=tuple(jax.ShapeDtypeStruct(g.shape, g.dtype) for g in grads),
        in_specs=[vmem] * 3,
        out_specs=(hbm, hbm, hbm),
        scratch_shapes=[dma((3,))],
        compiler_params=pltpu.CompilerParams(vmem_limit_bytes=24 * 1024 * 1024),
    )(*grads)


def solution(mesh):
    placed = (
        P("cp", None, "tp", None),
        P("cp", "tp", None),
        P("cp", "tp", None),
        P("cp", None, "tp", None),
        P(),
    )
    return jax.shard_map(
        functools.partial(per_device, mesh.shape["cp"], mesh.shape["tp"]),
        mesh=mesh,
        in_specs=placed,
        out_specs=(P("cp", None, "tp", None), P("cp", "tp", None), P("cp", "tp", None)),
        check_vma=False,
    )
```
